128 devices in a mesh: rep: 16 (over y_hi, z, core), seq: 8 (over x, y_lo).
Axes of the slice: x: 4, y: 4 (y_hi: 2, y_lo: 2; y = y_hi * 2 + y_lo), z: 4, core: 2. Of those that a mesh axis runs over, the one named last changes fastest.
Arguments:
- latent: bfloat16 [1536, 2432], P(('seq', 'rep')), may hold values from -50 to 50
- noise: bfloat16 [16, 1536, 2432], P('rep', 'seq'), may hold values from -6 to 6
- timestep: int32 [16], P('rep'), may hold values from 10 to 989
- text_kv: bfloat16 [2, 128, 1536], P(None, None, 'seq'), may hold values from -6 to 6
- qk_gain: float32 [2, 64], replicated, may hold values from 1 to 3
- prompt: float32 [1280], replicated, may hold values from -6 to 6
- w_qkv: bfloat16 [2432, 4608], P('rep'), may hold values from -0.125 to 0.125
- a_qkv: bfloat16 [2432, 64], replicated, may hold values from -0.125 to 0.125
- b_qkv: bfloat16 [64, 4608], replicated, may hold values from -0.75 to 0.75
- w_out: bfloat16 [1536, 2432], P('rep'), may hold values from -0.15625 to 0.15625
- a_out: bfloat16 [1536, 64], replicated, may hold values from -0.15625 to 0.15625
- b_out: bfloat16 [64, 2432], replicated, may hold values from -0.75 to 0.75
- w_patch: bfloat16 [2432, 1280], replicated, may hold values from -0.125 to 0.125
Outputs:
- rewards: float32 [16], P('rep')
- latent_grad: float32 [1536, 2432], P(('seq', 'rep'))
- grad_a_qkv: float32 [2432, 64], P('rep')
- grad_b_qkv: float32 [64, 4608], P(None, 'rep')
- grad_a_out: float32 [1536, 64], P('rep')
- grad_b_out: float32 [64, 2432], P(None, 'rep')
The draws below stay inside these ranges and needn't reach their ends.
All inputs are finite; a program needn't handle non-finite values.
Results may differ from the reference program's by a relative error of at most 0.024.
Values may be sent and summed in bfloat16 or wider, within the bound.
No kernel may reach another device: no remote copies, remote signals or barrier semaphores. Data moves between devices by JAX's collectives and lax.ppermute only.
A program may use at most 192 MiB of HBM per device.

```python
import math
import jax
import jax.numpy as jnp
from jax import lax

D = 2432
HEAD_DIM = 64
RANK = 64
VW = 1280
TXT = 128
HD = 1536
TOKENS = 1536
REPS = 16


def draw_latent(key, part):
    first, second = jax.random.split(key, 2)
    positions = jnp.arange(TOKENS, dtype=jnp.float32)
    rising = jnp.exp(jnp.log(3.0) * positions / TOKENS)
    jitter = jnp.exp(jax.random.uniform(first, (TOKENS,), minval=0.0, maxval=jnp.log(10.0 / 3.0)))
    row_scale = (rising * jitter)[:, None]
    values = jnp.clip(jax.random.normal(second, (TOKENS, D)), -4.0, 4.0)
    return (values * row_scale).astype(jnp.float32).astype(jnp.bfloat16)


def touch_ends(result, own_key, smallest, high):
    index_at = [jax.random.randint(jax.random.fold_in(own_key, axis), (), 0, length) for axis, length in enumerate(result.shape)]
    widest = result.shape.index(max(result.shape))
    beside = index_at[:widest] + [(index_at[widest] + 1) % result.shape[widest]] + index_at[widest + 1:]
    return result.at[tuple(index_at)].set(smallest).at[tuple(beside)].set(high)


def spiked(array, stream_key, source, target, blocks, factor):
    def block_of(position):
        return (jnp.arange(array.shape[position]) // (array.shape[position] // blocks)).reshape((-1,) + (1,) * (array.ndim - 1 - position))

    one_side = jax.random.permutation(stream_key, blocks)[block_of(target)]
    far = (block_of(target) + blocks // 2) % blocks
    return jnp.where((block_of(source) == one_side) | (block_of(source) == far), factor * array, array)


def level_of(key, shape, shards, smallest, top_value):
    def one(dim, blocks):
        steps = jax.random.uniform(jax.random.fold_in(jax.random.fold_in(key, 6), dim), (blocks,), jnp.float32, smallest / len(shards), top_value / len(shards))
        return jnp.repeat(jnp.exp(steps), shape[dim] // blocks).reshape((-1,) + (1,) * (len(shape) - dim - 1))

    level = one(*shards[0])
    for cut in shards[1:]:
        level = level * one(*cut)
    return level


def normal_values(stream_key, shape, spread, bound, pieces=(), kind=jnp.bfloat16):
    loudness = level_of(stream_key, shape, pieces, -0.22, 0.18) if pieces else 1.0
    entries = jax.random.normal(stream_key, shape, jnp.float32) * spread * loudness
    return jnp.minimum(jnp.maximum(entries, -bound), bound).astype(kind)


def heavy_noise(own_key, extent, width, reach, cuts, heavy, held_as=jnp.bfloat16):
    values = width * jax.random.normal(own_key, extent, jnp.float32)
    if cuts:
        values = values * level_of(own_key, extent, cuts, -0.22, 0.18)
    return jnp.clip(spiked(values, jax.random.fold_in(own_key, 3), *heavy), -reach, reach).astype(held_as)


def setup_inputs(seed: int = 0) -> dict:
    splits = jax.random.split(jax.random.key(seed), 14)
    latent = draw_latent(jax.random.fold_in(splits[13], 71), 0)
    noise = heavy_noise(splits[1], (REPS, TOKENS, D), 1.0, 6.0, ((0, 16), (1, 8)), (0, 1, 16, 2.0))
    timestep = touch_ends(jax.random.randint(splits[2], (REPS,), 10, 990), jax.random.fold_in(splits[2], 1), 10, 989).astype(jnp.int32)
    text_kv = normal_values(splits[3], (2, TXT, HD), 1.0, 6.0, ((2, 8),))
    qk_gain = jnp.clip(jnp.exp(jax.random.uniform(splits[4], (2, HEAD_DIM), jnp.float32, math.log(1.0), math.log(3.0))), 1.0, 3.0)
    prompt = normal_values(splits[5], (VW,), 1.0, 6.0, (), jnp.float32)
    w_qkv = normal_values(splits[6], (D, 3 * HD), D ** -0.5, 0.125, ((0, 16),))
    a_qkv = normal_values(splits[7], (D, RANK), D ** -0.5, 0.125)
    b_qkv = normal_values(splits[8], (RANK, 3 * HD), RANK ** -0.5, 0.75)
    w_out = normal_values(splits[9], (HD, D), HD ** -0.5, 0.15625, ((0, 16),))
    a_out = normal_values(splits[10], (HD, RANK), HD ** -0.5, 0.15625)
    b_out = normal_values(splits[11], (RANK, D), RANK ** -0.5, 0.75)
    w_patch = normal_values(splits[12], (D, VW), D ** -0.5, 0.125)
    return {"latent": latent, "noise": noise, "timestep": timestep, "text_kv": text_kv, "qk_gain": qk_gain, "prompt": prompt, "w_qkv": w_qkv, "a_qkv": a_qkv, "b_qkv": b_qkv, "w_out": w_out, "a_out": a_out, "b_out": b_out, "w_patch": w_patch}


epsilon = 1e-06
logit_scale = 100.0
contract_last = (((1,), (1,)), ((), ()))
contract_first = (((0,), (0,)), ((), ()))

def layer_norm(mixed_in):
    centred = mixed_in - lax.optimization_barrier(jnp.mean(mixed_in, axis=-1, keepdims=True))
    return centred * lax.rsqrt(lax.optimization_barrier(jnp.mean(centred * centred, axis=-1, keepdims=True)) + epsilon)

def head_norm(values_in, norm_gain, head_size):
    leading = values_in.shape[0]
    shaped = values_in.reshape(leading, -1, head_size)
    scaled = shaped * lax.rsqrt(lax.optimization_barrier(jnp.mean(shaped * shaped, axis=-1, keepdims=True)) + epsilon)
    return (scaled * norm_gain).reshape(leading, -1)

def split_heads(matrix, head_size):
    return jnp.transpose(matrix.reshape(matrix.shape[0], -1, head_size), (1, 0, 2))

def merge_heads(blocks):
    return jnp.transpose(blocks, (1, 0, 2)).reshape(blocks.shape[1], -1)

def project_in(latent_rows, noise_rows, noise_level, w_qkv, a_qkv, b_qkv, qk_gain, head_size):
    mixed_in = (1.0 - noise_level) * latent_rows.astype(jnp.float32) + noise_level * noise_rows.astype(jnp.float32)
    normed = layer_norm(mixed_in).astype(jnp.bfloat16)
    low_rank = jnp.dot(normed, a_qkv, preferred_element_type=jnp.float32).astype(jnp.bfloat16)
    joined_qkv = jnp.dot(normed, w_qkv, preferred_element_type=jnp.float32) + jnp.dot(low_rank, b_qkv, preferred_element_type=jnp.float32)
    inner_width = joined_qkv.shape[1] // 3
    query_part = head_norm(joined_qkv[:, :inner_width], qk_gain[0], head_size)
    key_part = head_norm(joined_qkv[:, inner_width:2 * inner_width], qk_gain[1], head_size)
    stacked = jnp.stack([query_part, key_part, joined_qkv[:, 2 * inner_width:]], axis=1).astype(jnp.bfloat16)
    return (mixed_in, normed, low_rank, joined_qkv, stacked)

def head_scores(query_head, key_head, head_size):
    logits = lax.dot_general(query_head, key_head, contract_last, preferred_element_type=jnp.float32) / math.sqrt(head_size)
    expped = jnp.exp(logits)
    return expped / lax.optimization_barrier(jnp.sum(expped, axis=1, keepdims=True))

def attend(stacked, text_keys, text_values, head_size):
    query_heads = split_heads(stacked[:, 0], head_size)
    key_heads = split_heads(jnp.concatenate([stacked[:, 1], text_keys], axis=0), head_size)
    value_heads = split_heads(jnp.concatenate([stacked[:, 2], text_values], axis=0), head_size)

    def one_head(inputs):
        query_head, key_head, value_head = inputs
        rounded = head_scores(query_head, key_head, head_size).astype(jnp.bfloat16)
        return jnp.dot(rounded, value_head, preferred_element_type=jnp.float32).astype(jnp.bfloat16)
    return merge_heads(lax.map(one_head, (query_heads, key_heads, value_heads)))

def attend_back(stacked, text_keys, text_values, grad_attended, head_size):
    tokens_all = stacked.shape[0]
    query_heads = split_heads(stacked[:, 0], head_size)
    key_heads = split_heads(jnp.concatenate([stacked[:, 1], text_keys], axis=0), head_size)
    value_heads = split_heads(jnp.concatenate([stacked[:, 2], text_values], axis=0), head_size)
    grad_heads = split_heads(grad_attended, head_size)

    def one_head(inputs):
        query_head, key_head, value_head, grad_head = inputs
        soft_probs = head_scores(query_head, key_head, head_size)
        rounded = soft_probs.astype(jnp.bfloat16)
        grad_values = lax.dot_general(rounded, grad_head, contract_first, preferred_element_type=jnp.float32)
        grad_probs = lax.dot_general(grad_head, value_head, contract_last, preferred_element_type=jnp.float32)
        centre = lax.optimization_barrier(jnp.sum(soft_probs * grad_probs, axis=1, keepdims=True))
        grad_logits = (soft_probs * (grad_probs - centre) / math.sqrt(head_size)).astype(jnp.bfloat16)
        grad_query = jnp.dot(grad_logits, key_head, preferred_element_type=jnp.float32)
        grad_keys = lax.dot_general(grad_logits, query_head, contract_first, preferred_element_type=jnp.float32)
        return jnp.stack([grad_query, grad_keys[:tokens_all], grad_values[:tokens_all]], axis=0)
    per_head = lax.map(one_head, (query_heads, key_heads, value_heads, grad_heads))
    return jnp.transpose(per_head, (2, 1, 0, 3)).reshape(tokens_all, 3, -1).astype(jnp.bfloat16)

def project_out(attended, mixed_in, noise_level, w_out, a_out, b_out, w_patch):
    low_out = jnp.dot(attended, a_out, preferred_element_type=jnp.float32).astype(jnp.bfloat16)
    velocity = jnp.dot(attended, w_out, preferred_element_type=jnp.float32) + jnp.dot(low_out, b_out, preferred_element_type=jnp.float32)
    denoised = (mixed_in - noise_level * velocity).astype(jnp.bfloat16)
    patch_pre = jnp.dot(denoised, w_patch, preferred_element_type=jnp.float32)
    return (low_out, patch_pre, lax.optimization_barrier(jnp.sum(jax.nn.gelu(patch_pre), axis=0)))

def reward(pooled, prompt):
    return logit_scale * jnp.sum(pooled * prompt) * lax.rsqrt(jnp.sum(pooled * pooled) + epsilon) * lax.rsqrt(jnp.sum(prompt * prompt) + epsilon)

def backward_out(patch_pre, grad_pooled, noise_level, attended, low_out, w_out, a_out, b_out, w_patch):
    gelu_back = jax.vjp(jax.nn.gelu, patch_pre)[1]
    grad_pre = gelu_back(jnp.broadcast_to(grad_pooled, patch_pre.shape))[0].astype(jnp.bfloat16)
    grad_denoised = lax.dot_general(grad_pre, w_patch, contract_last, preferred_element_type=jnp.float32)
    grad_velocity = (-noise_level * grad_denoised).astype(jnp.bfloat16)
    grad_low_out = lax.dot_general(grad_velocity, b_out, contract_last, preferred_element_type=jnp.float32).astype(jnp.bfloat16)
    grad_attended = (lax.dot_general(grad_velocity, w_out, contract_last, preferred_element_type=jnp.float32) + lax.dot_general(grad_low_out, a_out, contract_last, preferred_element_type=jnp.float32)).astype(jnp.bfloat16)
    grad_a_out = lax.dot_general(attended, grad_low_out, contract_first, preferred_element_type=jnp.float32)
    grad_b_out = lax.dot_general(low_out, grad_velocity, contract_first, preferred_element_type=jnp.float32)
    return (grad_denoised, grad_attended, grad_a_out, grad_b_out)

def backward_in(mixed_in, normed, low_rank, joined_qkv, grad_stacked, noise_level, w_qkv, a_qkv, b_qkv, qk_gain, head_size, grad_denoised):
    inner_width = joined_qkv.shape[1] // 3
    query_back = jax.vjp(lambda section: head_norm(section, qk_gain[0], head_size), joined_qkv[:, :inner_width])[1]
    key_back = jax.vjp(lambda section: head_norm(section, qk_gain[1], head_size), joined_qkv[:, inner_width:2 * inner_width])[1]
    grad_joined = jnp.concatenate([query_back(grad_stacked[:, 0].astype(jnp.float32))[0], key_back(grad_stacked[:, 1].astype(jnp.float32))[0], grad_stacked[:, 2].astype(jnp.float32)], axis=1).astype(jnp.bfloat16)
    grad_low = lax.dot_general(grad_joined, b_qkv, contract_last, preferred_element_type=jnp.float32).astype(jnp.bfloat16)
    grad_normed = lax.dot_general(grad_joined, w_qkv, contract_last, preferred_element_type=jnp.float32) + lax.dot_general(grad_low, a_qkv, contract_last, preferred_element_type=jnp.float32)
    grad_mixed = jax.vjp(layer_norm, mixed_in)[1](grad_normed)[0] + grad_denoised
    grad_latent = (1.0 - noise_level) * grad_mixed
    grad_a_qkv = lax.dot_general(normed, grad_low, contract_first, preferred_element_type=jnp.float32)
    grad_b_qkv = lax.dot_general(low_rank, grad_joined, contract_first, preferred_element_type=jnp.float32)
    return (grad_latent, grad_a_qkv, grad_b_qkv)

def reference(latent, noise, timestep, text_kv, qk_gain, prompt, w_qkv, a_qkv, b_qkv, w_out, a_out, b_out, w_patch):
    text_keys = head_norm(text_kv[0].astype(jnp.float32), qk_gain[1], HEAD_DIM).astype(jnp.bfloat16)
    text_values = text_kv[1]

    def replica(running, inputs):
        noise_rows, step_index = inputs
        noise_level = step_index.astype(jnp.float32) / 1000.0
        mixed_in, normed, low_rank, joined_qkv, stacked = project_in(latent, noise_rows, noise_level, w_qkv, a_qkv, b_qkv, qk_gain, HEAD_DIM)
        attended = attend(stacked, text_keys, text_values, HEAD_DIM)
        low_out, patch_pre, summed = project_out(attended, mixed_in, noise_level, w_out, a_out, b_out, w_patch)
        pooled = summed / TOKENS
        score_value, grad_pooled = jax.value_and_grad(reward)(pooled, prompt)
        grad_denoised, grad_attended, grad_a_out, grad_b_out = backward_out(patch_pre, grad_pooled, noise_level, attended, low_out, w_out, a_out, b_out, w_patch)
        grad_stacked = attend_back(stacked, text_keys, text_values, grad_attended, HEAD_DIM)
        grad_latent, grad_a_qkv, grad_b_qkv = backward_in(mixed_in, normed, low_rank, joined_qkv, grad_stacked, noise_level, w_qkv, a_qkv, b_qkv, qk_gain, HEAD_DIM, grad_denoised)
        updated = (running[0] + grad_latent, running[1] + grad_a_qkv, running[2] + grad_b_qkv, running[3] + grad_a_out, running[4] + grad_b_out)
        return (updated, score_value)
    initial = (jnp.zeros((TOKENS, D), jnp.float32), jnp.zeros((D, RANK), jnp.float32), jnp.zeros((RANK, 3 * HD), jnp.float32), jnp.zeros((HD, RANK), jnp.float32), jnp.zeros((RANK, D), jnp.float32))
    totals, rewards = lax.scan(replica, initial, (noise, timestep))
    return (rewards, totals[0], totals[1], totals[2], totals[3], totals[4])
```

```python
import math

import jax
import jax.numpy as jnp
from jax import lax
from jax.experimental import pallas as pl
from jax.experimental.pallas import tpu as pltpu
from jax.sharding import Mesh, PartitionSpec as P

HEAD_DIM = 64
CHIPS = ("yh", "z")
REP = ("yh", "z", "core")
SEQ = ("x", "yl")
QUERY_ROWS = 256
BACK_ROWS = 256


epsilon = 1e-06
logit_scale = 100.0
contract_last = (((1,), (1,)), ((), ()))
contract_first = (((0,), (0,)), ((), ()))


def layer_norm(mixed_in):
    centred = mixed_in - jnp.mean(mixed_in, axis=-1, keepdims=True)
    return centred * lax.rsqrt(jnp.mean(centred * centred, axis=-1, keepdims=True) + epsilon)


def head_norm(values_in, norm_gain, head_size):
    leading = values_in.shape[0]
    shaped = values_in.reshape(leading, -1, head_size)
    scaled = shaped * lax.rsqrt(jnp.mean(shaped * shaped, axis=-1, keepdims=True) + epsilon)
    return (scaled * norm_gain).reshape(leading, -1)


def mix_in(latent_rows, noise_rows, noise_level, a_qkv):
    mixed_in = (1.0 - noise_level) * latent_rows.astype(
        jnp.float32
    ) + noise_level * noise_rows.astype(jnp.float32)
    normed = layer_norm(mixed_in).astype(jnp.bfloat16)
    low_rank = jnp.dot(normed, a_qkv, preferred_element_type=jnp.float32).astype(jnp.bfloat16)
    return (mixed_in, normed, low_rank)


def head_scale(values, gain):
    return values * lax.rsqrt(jnp.mean(values * values, axis=-1, keepdims=True) + epsilon) * gain


def attend_kernel(order, near, far, text, gain, attended, queries, keys, values, widened):
    heads, latents = queries.shape[0], queries.shape[1]
    tokens, width = near.shape[0] // 4, near.shape[1] // 3
    texts = text.shape[1]
    widened[...] = jnp.zeros(widened.shape, jnp.bfloat16)
    for head in range(heads):
        left, right = head * HEAD_DIM, (head + 1) * HEAD_DIM
        for at in range(8):
            source, row = (near, far)[at // 4], (at % 4) * tokens
            rows = pl.ds(pl.multiple_of(order[at] * tokens, tokens), tokens)
            query = source[row : row + tokens, left:right]
            key = source[row : row + tokens, width + left : width + right]
            value = source[row : row + tokens, 2 * width + left : 2 * width + right]
            queries[head, rows, :] = head_scale(query, gain[0:1, :]).astype(jnp.bfloat16)
            keys[head, rows, :] = head_scale(key, gain[1:2, :]).astype(jnp.bfloat16)
            values[head, rows, :] = value.astype(jnp.bfloat16)
        text_key = text[0, :, left:right].astype(jnp.float32)
        keys[head, latents : latents + texts, :] = head_scale(text_key, gain[1:2, :]).astype(
            jnp.bfloat16
        )
        values[head, latents : latents + texts, :] = text[1, :, left:right]
        widened[head, :, 0:HEAD_DIM] = values[head]
        widened[head, :, HEAD_DIM : HEAD_DIM + 1] = jnp.ones((latents + texts, 1), jnp.bfloat16)

    def block(at, carry):
        rows = pl.ds(pl.multiple_of(at * QUERY_ROWS, QUERY_ROWS), QUERY_ROWS)
        parts = []
        for head in range(heads):
            logits = lax.dot_general(
                queries[head, rows, :], keys[head], contract_last, preferred_element_type=jnp.float32
            )
            expped = jnp.exp(logits * (1.0 / math.sqrt(HEAD_DIM))).astype(jnp.bfloat16)
            summed = jnp.dot(expped, widened[head], preferred_element_type=jnp.float32)
            parts.append(summed[:, :HEAD_DIM] / summed[:, HEAD_DIM : HEAD_DIM + 1])
        attended[rows, :] = jnp.concatenate(parts, axis=1).astype(jnp.bfloat16)
        return carry

    lax.fori_loop(0, latents // QUERY_ROWS, block, 0)


def attend_back_kernel(
    order,
    near,
    far,
    gain,
    queries,
    keys,
    values,
    attended,
    grads,
    grad_joined,
    key_columns,
    grad_queries,
    grad_keys,
    grad_values,
):
    heads, latents = queries.shape[0], queries.shape[1]
    tokens, width = near.shape[0] // 4, near.shape[1] // 3
    ones = jnp.ones((8, HEAD_DIM), jnp.float32)
    for head in range(heads):
        key_columns[head] = keys[head].astype(jnp.float32).T.astype(jnp.bfloat16)
    grad_keys[...] = jnp.zeros(grad_keys.shape, jnp.float32)
    grad_values[...] = jnp.zeros(grad_values.shape, jnp.float32)

    def block(at, carry):
        rows = pl.ds(pl.multiple_of(at * BACK_ROWS, BACK_ROWS), BACK_ROWS)
        for head in range(heads):
            left, right = head * HEAD_DIM, (head + 1) * HEAD_DIM
            query, grad = queries[head, rows, :], grads[rows, left:right]
            logits = lax.dot_general(
                keys[head], query, contract_last, preferred_element_type=jnp.float32
            )
            expped = jnp.exp(logits * (1.0 / math.sqrt(HEAD_DIM)))
            probs = expped * (1.0 / jnp.sum(expped, axis=0, keepdims=True))
            grad_probs = lax.dot_general(
                values[head], grad, contract_last, preferred_element_type=jnp.float32
            )
            products = attended[rows, left:right].astype(jnp.float32) * grad.astype(jnp.float32)
            centre = lax.dot_general(
                ones,
                products,
                contract_last,
                precision=lax.Precision.HIGHEST,
                preferred_element_type=jnp.float32,
            )[0:1, :]
            grad_logits = (probs * (grad_probs - centre)).astype(jnp.bfloat16)
            grad_values[head] += jnp.dot(
                probs[:latents].astype(jnp.bfloat16), grad, preferred_element_type=jnp.float32
            )
            grad_keys[head] += jnp.dot(
                grad_logits[:latents], query, preferred_element_type=jnp.float32
            )
            grad_queries[head, rows, :] = jnp.dot(
                key_columns[head], grad_logits, preferred_element_type=jnp.float32
            ).T
        return carry

    lax.fori_loop(0, latents // BACK_ROWS, block, 0)

    scale = 1.0 / math.sqrt(HEAD_DIM)
    for at in range(8):
        source, row = (near, far)[at // 4], (at % 4) * tokens
        rows = pl.ds(pl.multiple_of(order[at] * tokens, tokens), tokens)
        parts = []
        for part, sums in enumerate((grad_queries, grad_keys)):
            for head in range(heads):
                left = part * width + head * HEAD_DIM
                inputs = source[row : row + tokens, left : left + HEAD_DIM]
                incoming = (sums[head, rows, :] * scale).astype(jnp.bfloat16).astype(jnp.float32)
                incoming = incoming * gain[part : part + 1, :]
                inverse = lax.rsqrt(jnp.mean(inputs * inputs, axis=-1, keepdims=True) + epsilon)
                along = jnp.mean(inputs * incoming, axis=-1, keepdims=True)
                parts.append(inverse * incoming - inputs * (inverse * inverse * inverse * along))
        for head in range(heads):
            parts.append(grad_values[head, rows, :])
        grad_joined[rows, :] = jnp.concatenate(parts, axis=1).astype(jnp.bfloat16)


def in_vmem(count):
    return [pl.BlockSpec(memory_space=pltpu.VMEM)] * count


def attend(order, near, far, text_kv, qk_gain):
    latents, heads = 2 * near.shape[0], near.shape[1] // (3 * HEAD_DIM)
    everything = latents + text_kv.shape[1]
    return pl.pallas_call(
        attend_kernel,
        name="attend",
        out_shape=(
            jax.ShapeDtypeStruct((latents, heads * HEAD_DIM), jnp.bfloat16),
            jax.ShapeDtypeStruct((heads, latents, HEAD_DIM), jnp.bfloat16),
            jax.ShapeDtypeStruct((heads, everything, HEAD_DIM), jnp.bfloat16),
            jax.ShapeDtypeStruct((heads, everything, HEAD_DIM), jnp.bfloat16),
        ),
        in_specs=[pl.BlockSpec(memory_space=pltpu.SMEM)] + in_vmem(4),
        out_specs=tuple(in_vmem(4)),
        scratch_shapes=[pltpu.VMEM((heads, everything, 2 * HEAD_DIM), jnp.bfloat16)],
    )(order, near, far, text_kv, qk_gain)


def attend_back(order, near, far, qk_gain, queries, keys, values, attended, grads):
    heads, latents = queries.shape[0], queries.shape[1]
    return pl.pallas_call(
        attend_back_kernel,
        name="attend_back",
        out_shape=jax.ShapeDtypeStruct((latents, near.shape[1]), jnp.bfloat16),
        in_specs=[pl.BlockSpec(memory_space=pltpu.SMEM)] + in_vmem(8),
        out_specs=pl.BlockSpec(memory_space=pltpu.VMEM),
        scratch_shapes=[
            pltpu.VMEM((heads, HEAD_DIM, keys.shape[1]), jnp.bfloat16),
            pltpu.VMEM((heads, latents, HEAD_DIM), jnp.float32),
            pltpu.VMEM((heads, latents, HEAD_DIM), jnp.float32),
            pltpu.VMEM((heads, latents, HEAD_DIM), jnp.float32),
        ],
    )(order, near, far, qk_gain, queries, keys, values, attended, grads)


def project_out(attended, mixed_in, noise_level, w_out, a_out, b_out, w_patch):
    low_out = jnp.dot(attended, a_out, preferred_element_type=jnp.float32).astype(jnp.bfloat16)
    velocity = jnp.dot(attended, w_out, preferred_element_type=jnp.float32) + jnp.dot(
        low_out, b_out, preferred_element_type=jnp.float32
    )
    denoised = (mixed_in - noise_level * velocity).astype(jnp.bfloat16)
    patch_pre = jnp.dot(denoised, w_patch, preferred_element_type=jnp.float32)
    return (low_out, patch_pre, jnp.sum(jax.nn.gelu(patch_pre), axis=0))


def reward(pooled, prompt):
    return (
        logit_scale
        * jnp.sum(pooled * prompt)
        * lax.rsqrt(jnp.sum(pooled * pooled) + epsilon)
        * lax.rsqrt(jnp.sum(prompt * prompt) + epsilon)
    )


def backward_out(
    patch_pre, grad_pooled, noise_level, attended, low_out, w_out, a_out, b_out, w_patch
):
    gelu_back = jax.vjp(jax.nn.gelu, patch_pre)[1]
    grad_pre = gelu_back(jnp.broadcast_to(grad_pooled, patch_pre.shape))[0].astype(jnp.bfloat16)
    grad_denoised = lax.dot_general(
        grad_pre, w_patch, contract_last, preferred_element_type=jnp.float32
    )
    grad_velocity = (-noise_level * grad_denoised).astype(jnp.bfloat16)
    grad_low_out = lax.dot_general(
        grad_velocity, b_out, contract_last, preferred_element_type=jnp.float32
    ).astype(jnp.bfloat16)
    grad_attended = (
        lax.dot_general(grad_velocity, w_out, contract_last, preferred_element_type=jnp.float32)
        + lax.dot_general(grad_low_out, a_out, contract_last, preferred_element_type=jnp.float32)
    ).astype(jnp.bfloat16)
    grad_a_out = lax.dot_general(
        attended, grad_low_out, contract_first, preferred_element_type=jnp.float32
    )
    grad_b_out = lax.dot_general(
        grad_velocity, low_out, contract_first, preferred_element_type=jnp.float32
    )
    return (grad_denoised, grad_attended, grad_a_out, grad_b_out)


def shift(block, axis, step, size):
    return lax.ppermute(block, axis, [(i, (i + step) % size) for i in range(size)])


def exchange(blocks, axes):
    return lax.all_to_all(blocks, axes, split_axis=0, concat_axis=0, tiled=True)


def spread(block, axes, size):
    return exchange(jnp.broadcast_to(block[None], (size,) + block.shape), axes)


def gather_rep(block):
    mine = spread(block, CHIPS, 8)
    other = shift(mine, "core", 1, 2)
    first_core = lax.axis_index("core") == 0
    pair = jnp.stack(
        [jnp.where(first_core, mine, other), jnp.where(first_core, other, mine)], axis=1
    )
    return pair.reshape((16 * block.shape[0],) + block.shape[1:])


def scatter_rep(chunks):
    pairs = chunks.reshape((8, 2) + chunks.shape[1:])
    core = lax.axis_index("core")
    mine = lax.dynamic_index_in_dim(pairs, core, 1, keepdims=False)
    other = lax.dynamic_index_in_dim(pairs, 1 - core, 1, keepdims=False)
    got = shift(other.astype(jnp.bfloat16), "core", 1, 2)
    both = (mine.astype(jnp.float32) + got.astype(jnp.float32)).astype(jnp.bfloat16)
    return jnp.sum(exchange(both, CHIPS).astype(jnp.float32), axis=0)


def sum_seq(block):
    return jnp.sum(spread(block.astype(jnp.bfloat16), SEQ, 8).astype(jnp.float32), axis=0)


def joined_all(rows, weight):
    half = rows.shape[0] // 2
    before = shift(rows, "x", 1, 4)
    after = shift(rows, "x", -1, 4)
    beside = shift(rows, "yl", 1, 2)
    before_beside = shift(beside, "x", 1, 4)
    after_beside = shift(beside, "x", -1, 4)
    far_top = shift(before[:half], "x", 1, 4)
    far_low = shift(after[half:], "x", -1, 4)
    far_beside_top = shift(before_beside[:half], "x", 1, 4)
    far_beside_low = shift(after_beside[half:], "x", -1, 4)
    near = jnp.concatenate([rows, before, after, beside], axis=0)
    far = jnp.concatenate(
        [before_beside, after_beside, far_top, far_low, far_beside_top, far_beside_low], axis=0
    )
    at_x, at_y = lax.axis_index("x"), lax.axis_index("yl")
    steps = ((0, 0), (3, 0), (1, 0), (0, 1), (3, 1), (1, 1), (2, 0), (2, 1))
    order = jnp.stack([((at_x + x) % 4) * 2 + (at_y + y) % 2 for x, y in steps])
    return (
        jnp.dot(near, weight, preferred_element_type=jnp.float32),
        jnp.dot(far, weight, preferred_element_type=jnp.float32),
        order.astype(jnp.int32),
    )


def by_group(columns):
    rows = columns.shape[0]
    return jnp.transpose(columns.reshape(rows, 3, 8, -1), (0, 2, 1, 3)).reshape(rows, -1)


def shards(
    latent,
    noise,
    timestep,
    text_kv,
    qk_gain,
    prompt,
    w_qkv,
    a_qkv,
    b_qkv,
    w_out,
    a_out,
    b_out,
    w_patch,
):
    group = lax.axis_index("x") * 2 + lax.axis_index("yl")
    inner_width, own_width = w_qkv.shape[1] // 3, w_qkv.shape[1] // 24

    def own_columns(matrix):
        return jnp.concatenate(
            [
                lax.dynamic_slice_in_dim(
                    matrix, part * inner_width + group * own_width, own_width, 1
                )
                for part in range(3)
            ],
            axis=1,
        )

    weight_mine = lax.all_gather(own_columns(w_qkv), REP, axis=0, tiled=True)
    latent_rows = gather_rep(latent)
    w_out, latent_rows = lax.optimization_barrier((w_out, latent_rows))
    weight_back = lax.all_gather(w_out, REP, axis=0, tiled=True)

    noise_level = timestep[0].astype(jnp.float32) / 1000.0
    mixed_in, normed, low_rank = mix_in(latent_rows, noise[0], noise_level, a_qkv)
    w_later, normed = lax.optimization_barrier((w_qkv, normed))
    weight_in = lax.all_gather(by_group(w_later), REP, axis=0, tiled=True)
    b_grouped = by_group(b_qkv)
    near, far, order = joined_all(
        jnp.concatenate([normed, low_rank], axis=1),
        jnp.concatenate([weight_mine, own_columns(b_qkv)], axis=0),
    )
    attended_heads, queries, keys, values = attend(order, near, far, text_kv, qk_gain)
    tokens = mixed_in.shape[0]
    attended = exchange(attended_heads.reshape(8, tokens, -1), SEQ)
    attended = jnp.transpose(attended, (1, 0, 2)).reshape(tokens, -1)
    low_out, patch_pre, partial_sum = project_out(
        attended, mixed_in, noise_level, weight_back, a_out, b_out, w_patch
    )
    summed = jnp.sum(spread(partial_sum, SEQ, 8), axis=0)
    pooled = summed / (tokens * 8)
    score_value, grad_pooled = jax.value_and_grad(reward)(pooled, prompt)
    grad_denoised, grad_attended, grad_a_out, grad_b_out = backward_out(
        patch_pre, grad_pooled, noise_level, attended, low_out, weight_back, a_out, b_out, w_patch
    )
    grad_heads = exchange(
        jnp.transpose(grad_attended.reshape(tokens, 8, -1), (1, 0, 2)), SEQ
    ).reshape(8 * tokens, -1)
    out_chunks = jnp.concatenate(
        [
            jnp.pad(grad_a_out.reshape(16, 96, 64), ((0, 0), (0, 56), (0, 0))),
            grad_b_out.reshape(16, 152, 64),
        ],
        axis=2,
    )
    out_shard = sum_seq(scatter_rep(out_chunks))
    grad_joined = attend_back(
        order, near, far, qk_gain, queries, keys, values, attended_heads, grad_heads
    )
    grad_joined = exchange(grad_joined.reshape(8, tokens, -1), SEQ)
    grad_joined = jnp.transpose(grad_joined, (1, 0, 2)).reshape(tokens, -1)

    grad_low = lax.dot_general(
        grad_joined, b_grouped, contract_last, preferred_element_type=jnp.float32
    ).astype(jnp.bfloat16)
    grad_normed = lax.dot_general(
        grad_joined, weight_in, contract_last, preferred_element_type=jnp.float32
    ) + lax.dot_general(grad_low, a_qkv, contract_last, preferred_element_type=jnp.float32)
    grad_mixed = jax.vjp(layer_norm, mixed_in)[1](grad_normed)[0] + grad_denoised
    grad_latent = (1.0 - noise_level) * grad_mixed
    grad_a_qkv = lax.dot_general(
        normed, grad_low, contract_first, preferred_element_type=jnp.float32
    )
    grad_b_qkv = lax.dot_general(
        grad_joined, low_rank, contract_first, preferred_element_type=jnp.float32
    )
    grad_b_qkv = jnp.transpose(grad_b_qkv.reshape(8, 3, 192, 64), (1, 0, 2, 3)).reshape(16, 288, 64)
    in_chunks = jnp.concatenate(
        [
            jnp.concatenate([grad_a_qkv.reshape(16, 152, 64), grad_b_qkv[:, :152]], axis=2),
            jnp.concatenate([grad_b_qkv[:, 152:], grad_b_qkv[:, 152:]], axis=2),
        ],
        axis=1,
    )
    in_shard = sum_seq(scatter_rep(in_chunks))
    latent_chunks = jnp.pad(grad_latent.reshape(16, 12, -1), ((0, 0), (0, 4), (0, 0)))
    latent_grad = scatter_rep(latent_chunks)[:12]
    shard_b_qkv = jnp.concatenate([in_shard[:152, 64:], in_shard[152:, :64]], axis=0).T
    return (
        score_value.reshape(1),
        latent_grad,
        in_shard[:152, :64],
        shard_b_qkv,
        out_shard[:96, :64],
        out_shard[:, 64:].T,
    )


def solution(mesh):
    parts = Mesh(mesh.devices.reshape(2, 4, 2, 4, 2), ("yh", "z", "core", "x", "yl"))
    in_specs = (
        P(SEQ + REP, None),
        P(REP, SEQ, None),
        P(REP),
        P(None, None, SEQ),
        P(),
        P(),
        P(REP, None),
        P(),
        P(),
        P(REP, None),
        P(),
        P(),
        P(),
    )
    out_specs = (
        P(REP),
        P(SEQ + REP, None),
        P(REP, None),
        P(None, REP),
        P(REP, None),
        P(None, REP),
    )
    return jax.shard_map(shards, mesh=parts, in_specs=in_specs, out_specs=out_specs, check_vma=False)
```

```python
import math

import jax
import jax.numpy as jnp
from jax import lax
from jax.experimental import pallas as pl
from jax.experimental.pallas import tpu as pltpu
from jax.sharding import Mesh, PartitionSpec as P

HEAD_DIM = 64
CHIPS = ("yh", "z")
REP = ("yh", "z", "core")
SEQ = ("x", "yl")
QUERY_ROWS = 256
BACK_ROWS = 256
DOWN_ROWS = 80


epsilon = 1e-06
logit_scale = 100.0
contract_last = (((1,), (1,)), ((), ()))
contract_first = (((0,), (0,)), ((), ()))


def layer_norm(mixed_in):
    centred = mixed_in - jnp.mean(mixed_in, axis=-1, keepdims=True)
    return centred * lax.rsqrt(jnp.mean(centred * centred, axis=-1, keepdims=True) + epsilon)


def mix_in(latent_rows, noise_rows, noise_level):
    mixed_in = (1.0 - noise_level) * latent_rows.astype(
        jnp.float32
    ) + noise_level * noise_rows.astype(jnp.float32)
    normed = layer_norm(mixed_in).astype(jnp.bfloat16)
    return (mixed_in, normed)


def head_scale(values, gain):
    return values * lax.rsqrt(jnp.mean(values * values, axis=-1, keepdims=True) + epsilon) * gain


def block_rows(sources, tokens):
    return [(ref, row) for ref in sources for row in range(0, ref.shape[0], tokens)]


def attend_kernel(
    order,
    near,
    middle,
    last,
    up,
    text,
    gain,
    attended,
    queries,
    keys,
    values,
    joined,
    lows,
    widened,
):
    heads, latents = queries.shape[0], queries.shape[1]
    tokens, width = last.shape[0], joined.shape[1] // 3
    texts = text.shape[1]
    widened[...] = jnp.zeros(widened.shape, jnp.bfloat16)
    for at, (source, row) in enumerate(block_rows((near, middle, last), tokens)):
        rows = pl.ds(pl.multiple_of(order[at] * tokens, tokens), tokens)
        low = source[row : row + tokens, 3 * width :].astype(jnp.bfloat16)
        block = source[row : row + tokens, : 3 * width] + jnp.dot(
            low, up[...], preferred_element_type=jnp.float32
        )
        joined[rows, :] = block
        lows[rows, :] = low
        for head in range(heads):
            left, right = head * HEAD_DIM, (head + 1) * HEAD_DIM
            query, key = block[:, left:right], block[:, width + left : width + right]
            value = block[:, 2 * width + left : 2 * width + right]
            queries[head, rows, :] = head_scale(query, gain[0:1, :]).astype(jnp.bfloat16)
            keys[head, rows, :] = head_scale(key, gain[1:2, :]).astype(jnp.bfloat16)
            values[head, rows, :] = value.astype(jnp.bfloat16)
    for head in range(heads):
        left, right = head * HEAD_DIM, (head + 1) * HEAD_DIM
        text_key = text[0, :, left:right].astype(jnp.float32)
        keys[head, latents : latents + texts, :] = head_scale(text_key, gain[1:2, :]).astype(
            jnp.bfloat16
        )
        values[head, latents : latents + texts, :] = text[1, :, left:right]
        widened[head, :, 0:HEAD_DIM] = values[head]
        widened[head, :, HEAD_DIM : HEAD_DIM + 1] = jnp.ones((latents + texts, 1), jnp.bfloat16)

    def block(at, carry):
        rows = pl.ds(pl.multiple_of(at * QUERY_ROWS, QUERY_ROWS), QUERY_ROWS)
        parts = []
        for head in range(heads):
            logits = lax.dot_general(
                queries[head, rows, :], keys[head], contract_last, preferred_element_type=jnp.float32
            )
            expped = jnp.exp(logits * (1.0 / math.sqrt(HEAD_DIM))).astype(jnp.bfloat16)
            summed = jnp.dot(expped, widened[head], preferred_element_type=jnp.float32)
            parts.append(summed[:, :HEAD_DIM] / summed[:, HEAD_DIM : HEAD_DIM + 1])
        attended[rows, :] = jnp.concatenate(parts, axis=1).astype(jnp.bfloat16)
        return carry

    lax.fori_loop(0, latents // QUERY_ROWS, block, 0)


def attend_back_kernel(
    group,
    joined,
    lows,
    gain,
    queries,
    keys,
    values,
    attended,
    grads,
    grad_a_out,
    grad_b_out,
    grad_joined,
    chunks,
    key_columns,
    grad_queries,
    grad_keys,
    grad_values,
):
    heads, latents = queries.shape[0], queries.shape[1]
    tokens, width, rank = latents // 8, joined.shape[1] // 3, lows.shape[1]
    ones = jnp.ones((8, HEAD_DIM), jnp.float32)
    for head in range(heads):
        key_columns[head] = keys[head].astype(jnp.float32).T.astype(jnp.bfloat16)
    grad_keys[...] = jnp.zeros(grad_keys.shape, jnp.float32)
    grad_values[...] = jnp.zeros(grad_values.shape, jnp.float32)

    def block(at, carry):
        rows = pl.ds(pl.multiple_of(at * BACK_ROWS, BACK_ROWS), BACK_ROWS)
        for head in range(heads):
            left, right = head * HEAD_DIM, (head + 1) * HEAD_DIM
            query, grad = queries[head, rows, :], grads[rows, left:right]
            logits = lax.dot_general(
                keys[head], query, contract_last, preferred_element_type=jnp.float32
            )
            expped = jnp.exp(logits * (1.0 / math.sqrt(HEAD_DIM)))
            probs = expped * (1.0 / jnp.sum(expped, axis=0, keepdims=True))
            grad_probs = lax.dot_general(
                values[head], grad, contract_last, preferred_element_type=jnp.float32
            )
            products = attended[rows, left:right].astype(jnp.float32) * grad.astype(jnp.float32)
            centre = lax.dot_general(
                ones,
                products,
                contract_last,
                precision=lax.Precision.HIGHEST,
                preferred_element_type=jnp.float32,
            )[0:1, :]
            grad_logits = (probs * (grad_probs - centre)).astype(jnp.bfloat16)
            grad_values[head] += jnp.dot(
                probs[:latents].astype(jnp.bfloat16), grad, preferred_element_type=jnp.float32
            )
            grad_keys[head] += jnp.dot(
                grad_logits[:latents], query, preferred_element_type=jnp.float32
            )
            grad_queries[head, rows, :] = jnp.dot(
                key_columns[head], grad_logits, preferred_element_type=jnp.float32
            ).T
        return carry

    lax.fori_loop(0, latents // BACK_ROWS, block, 0)

    scale = 1.0 / math.sqrt(HEAD_DIM)
    grad_up = jnp.zeros((3 * width, rank), jnp.float32)
    for at in range(8):
        rows = slice(at * tokens, (at + 1) * tokens)
        parts = []
        for part, sums in enumerate((grad_queries, grad_keys)):
            for head in range(heads):
                left = part * width + head * HEAD_DIM
                inputs = joined[rows, left : left + HEAD_DIM]
                incoming = (sums[head, rows, :] * scale).astype(jnp.bfloat16).astype(jnp.float32)
                incoming = incoming * gain[part : part + 1, :]
                inverse = lax.rsqrt(jnp.mean(inputs * inputs, axis=-1, keepdims=True) + epsilon)
                along = jnp.mean(inputs * incoming, axis=-1, keepdims=True)
                parts.append(inverse * incoming - inputs * (inverse * inverse * inverse * along))
        for head in range(heads):
            parts.append(grad_values[head, rows, :])
        block = jnp.concatenate(parts, axis=1).astype(jnp.bfloat16)
        grad_up += lax.dot_general(
            block, lows[rows, :], contract_first, preferred_element_type=jnp.float32
        )
        spare = grad_joined.shape[1] - block.shape[1]
        grad_joined[rows, :] = jnp.concatenate(
            [block, jnp.zeros((tokens, spare), jnp.bfloat16)], axis=1
        )

    chunks[...] = jnp.zeros(chunks.shape, jnp.bfloat16)
    for part in range(3):
        place = pl.ds(pl.multiple_of(part * latents + group[0] * width, width), width)
        chunks[place, 0:rank] = grad_up[part * width : (part + 1) * width].astype(jnp.bfloat16)
    size, first, second = (ref.shape[0] // 16 for ref in (chunks, grad_a_out, grad_b_out))
    for replica in range(16):
        at = replica * size
        chunks[at : at + first, rank:] = grad_a_out[
            replica * first : (replica + 1) * first, :
        ].astype(jnp.bfloat16)
        chunks[at + first : at + first + second, rank:] = grad_b_out[
            replica * second : (replica + 1) * second, :
        ].astype(jnp.bfloat16)


def low_back_kernel(grad_joined, up, normed, flat, grad_low, grad_down):
    groups, tokens, width = grad_joined.shape
    total = jnp.zeros((tokens, up.shape[0]), jnp.float32)
    for group in range(groups):
        columns = slice(group * width, (group + 1) * width)
        flat[:, columns] = grad_joined[group]
        total += lax.dot_general(
            grad_joined[group], up[:, columns], contract_last, preferred_element_type=jnp.float32
        )
    low = total.astype(jnp.bfloat16)
    grad_low[...] = low
    down = lax.dot_general(normed[...], low, contract_first, preferred_element_type=jnp.float32)
    replicas, rows, lanes = grad_down.shape
    size, rank = down.shape[0] // replicas, down.shape[1]
    grad_down[...] = jnp.zeros(grad_down.shape, jnp.float32)
    for replica in range(replicas):
        at = replica * size
        grad_down[replica, :, 0:rank] = down[at : at + rows]
        grad_down[replica, 0 : size - rows, rank:lanes] = down[at + rows : at + size]


def in_vmem(count):
    return [pl.BlockSpec(memory_space=pltpu.VMEM)] * count


def attend(order, sources, up, text_kv, qk_gain):
    latents, rank, width = 8 * sources[-1].shape[0], up.shape[0], up.shape[1]
    heads = width // (3 * HEAD_DIM)
    everything = latents + text_kv.shape[1]
    return pl.pallas_call(
        attend_kernel,
        name="attend",
        out_shape=(
            jax.ShapeDtypeStruct((latents, heads * HEAD_DIM), jnp.bfloat16),
            jax.ShapeDtypeStruct((heads, latents, HEAD_DIM), jnp.bfloat16),
            jax.ShapeDtypeStruct((heads, everything, HEAD_DIM), jnp.bfloat16),
            jax.ShapeDtypeStruct((heads, everything, HEAD_DIM), jnp.bfloat16),
            jax.ShapeDtypeStruct((latents, width), jnp.float32),
            jax.ShapeDtypeStruct((latents, rank), jnp.bfloat16),
        ),
        in_specs=[pl.BlockSpec(memory_space=pltpu.SMEM)] + in_vmem(6),
        out_specs=tuple(in_vmem(6)),
        scratch_shapes=[pltpu.VMEM((heads, everything, 2 * HEAD_DIM), jnp.bfloat16)],
    )(order, *sources, up, text_kv, qk_gain)


def attend_back(group, joined, lows, qk_gain, queries, keys, values, attended, grads, out_grads):
    heads, latents, rank = queries.shape[0], queries.shape[1], lows.shape[1]
    width = joined.shape[1]
    return pl.pallas_call(
        attend_back_kernel,
        name="attend_back",
        out_shape=(
            jax.ShapeDtypeStruct((latents, pl.cdiv(width, 128) * 128), jnp.bfloat16),
            jax.ShapeDtypeStruct((8 * width, 2 * rank), jnp.bfloat16),
        ),
        in_specs=[pl.BlockSpec(memory_space=pltpu.SMEM)] + in_vmem(10),
        out_specs=tuple(in_vmem(2)),
        scratch_shapes=[
            pltpu.VMEM((heads, HEAD_DIM, keys.shape[1]), jnp.bfloat16),
            pltpu.VMEM((heads, latents, HEAD_DIM), jnp.float32),
            pltpu.VMEM((heads, latents, HEAD_DIM), jnp.float32),
            pltpu.VMEM((heads, latents, HEAD_DIM), jnp.float32),
        ],
    )(group, joined, lows, qk_gain, queries, keys, values, attended, grads, *out_grads)


def low_back(grad_joined, up, normed):
    groups, tokens, width = grad_joined.shape
    return pl.pallas_call(
        low_back_kernel,
        name="low_back",
        out_shape=(
            jax.ShapeDtypeStruct((tokens, groups * width), jnp.bfloat16),
            jax.ShapeDtypeStruct((tokens, up.shape[0]), jnp.bfloat16),
            jax.ShapeDtypeStruct((16, DOWN_ROWS, 2 * up.shape[0]), jnp.float32),
        ),
        in_specs=in_vmem(3),
        out_specs=tuple(in_vmem(3)),
    )(grad_joined, up, normed)


def project_out(attended, mixed_in, noise_level, w_out, a_out, b_out, w_patch):
    low_out = jnp.dot(attended, a_out, preferred_element_type=jnp.float32).astype(jnp.bfloat16)
    velocity = jnp.dot(attended, w_out, preferred_element_type=jnp.float32) + jnp.dot(
        low_out, b_out, preferred_element_type=jnp.float32
    )
    denoised = (mixed_in - noise_level * velocity).astype(jnp.bfloat16)
    patch_pre = jnp.dot(denoised, w_patch, preferred_element_type=jnp.float32)
    return (low_out, patch_pre, jnp.sum(jax.nn.gelu(patch_pre), axis=0))


def reward(pooled, prompt):
    return (
        logit_scale
        * jnp.sum(pooled * prompt)
        * lax.rsqrt(jnp.sum(pooled * pooled) + epsilon)
        * lax.rsqrt(jnp.sum(prompt * prompt) + epsilon)
    )


def backward_out(
    patch_pre, grad_pooled, noise_level, attended, low_out, w_out, a_out, b_out, w_patch
):
    gelu_back = jax.vjp(jax.nn.gelu, patch_pre)[1]
    grad_pre = gelu_back(jnp.broadcast_to(grad_pooled, patch_pre.shape))[0].astype(jnp.bfloat16)
    grad_denoised = lax.dot_general(
        grad_pre, w_patch, contract_last, preferred_element_type=jnp.float32
    )
    grad_velocity = (-noise_level * grad_denoised).astype(jnp.bfloat16)
    grad_low_out = lax.dot_general(
        grad_velocity, b_out, contract_last, preferred_element_type=jnp.float32
    ).astype(jnp.bfloat16)
    grad_attended = (
        lax.dot_general(grad_velocity, w_out, contract_last, preferred_element_type=jnp.float32)
        + lax.dot_general(grad_low_out, a_out, contract_last, preferred_element_type=jnp.float32)
    ).astype(jnp.bfloat16)
    grad_a_out = lax.dot_general(
        attended, grad_low_out, contract_first, preferred_element_type=jnp.float32
    )
    grad_b_out = lax.dot_general(
        grad_velocity, low_out, contract_first, preferred_element_type=jnp.float32
    )
    return (grad_denoised, grad_attended, grad_a_out, grad_b_out)


def shift(block, axis, step, size):
    return lax.ppermute(block, axis, [(i, (i + step) % size) for i in range(size)])


def exchange(blocks, axes):
    return lax.all_to_all(blocks, axes, split_axis=0, concat_axis=0, tiled=True)


def spread(block, axes, size):
    return exchange(jnp.broadcast_to(block[None], (size,) + block.shape), axes)


def gather_rep(block):
    mine = spread(block, CHIPS, 8)
    other = shift(mine, "core", 1, 2)
    first_core = lax.axis_index("core") == 0
    pair = jnp.stack(
        [jnp.where(first_core, mine, other), jnp.where(first_core, other, mine)], axis=1
    )
    return pair.reshape((16 * block.shape[0],) + block.shape[1:])


def halve(chunks):
    pairs = chunks.reshape((8, 2) + chunks.shape[1:])
    core = lax.axis_index("core")
    mine = lax.dynamic_index_in_dim(pairs, core, 1, keepdims=False)
    other = lax.dynamic_index_in_dim(pairs, 1 - core, 1, keepdims=False)
    got = shift(other.astype(jnp.bfloat16), "core", 1, 2)
    return (mine.astype(jnp.float32) + got.astype(jnp.float32)).astype(jnp.bfloat16)


def scatter_chips(half):
    parts = exchange(half, CHIPS)
    return jnp.sum(parts.astype(jnp.float32), axis=0)


def sum_seq(block):
    for axis, size, distance in (("yl", 2, 1), ("x", 4, 1), ("x", 4, 2)):
        sent = block.astype(jnp.bfloat16)
        got = lax.ppermute(sent, axis, [(i, i ^ distance) for i in range(size)])
        block = sent.astype(jnp.float32) + got.astype(jnp.float32)
    return block


def joined_all(rows, weight):
    third = rows.shape[0] // 3
    before = shift(rows, "x", 1, 4)
    after = shift(rows, "x", -1, 4)
    beside = shift(rows, "yl", 1, 2)
    before, after, beside = lax.optimization_barrier((before, after, beside))
    far = shift(before, "x", 1, 4)
    after_beside = shift(beside, "x", -1, 4)
    before_beside = shift(before, "yl", 1, 2)
    near = jnp.concatenate([rows, before, after, beside], axis=0)
    near = jnp.dot(near, weight, preferred_element_type=jnp.float32)
    far, after_beside, before_beside, near = lax.optimization_barrier(
        (far, after_beside, before_beside, near)
    )
    opposite = [
        shift(before_beside[:third], "x", 1, 4),
        shift(after_beside[third : 2 * third], "x", -1, 4),
        shift(far[2 * third :], "yl", 1, 2),
    ]
    middle = jnp.concatenate([far, after_beside, before_beside], axis=0)
    middle = jnp.dot(middle, weight, preferred_element_type=jnp.float32)
    *opposite, middle = lax.optimization_barrier((*opposite, middle))
    last = jnp.concatenate(opposite, axis=0)
    last = jnp.dot(last, weight, preferred_element_type=jnp.float32)
    at_x, at_y = lax.axis_index("x"), lax.axis_index("yl")
    steps = ((0, 0), (3, 0), (1, 0), (0, 1), (2, 0), (1, 1), (3, 1), (2, 1))
    order = jnp.stack([((at_x + x) % 4) * 2 + (at_y + y) % 2 for x, y in steps])
    return ((near, middle, last), order.astype(jnp.int32))


def by_group(columns):
    rows = columns.shape[0]
    grouped = jnp.transpose(columns.reshape(rows, 3, 8, -1), (0, 2, 1, 3)).reshape(rows, 8, -1)
    spare = -grouped.shape[2] % 128
    return jnp.pad(grouped, ((0, 0), (0, 0), (0, spare))).reshape(rows, -1)


def shards(
    latent,
    noise,
    timestep,
    text_kv,
    qk_gain,
    prompt,
    w_qkv,
    a_qkv,
    b_qkv,
    w_out,
    a_out,
    b_out,
    w_patch,
):
    group = lax.axis_index("x") * 2 + lax.axis_index("yl")
    inner_width, own_width = w_qkv.shape[1] // 3, w_qkv.shape[1] // 24

    def own_columns(matrix):
        return jnp.concatenate(
            [
                lax.dynamic_slice_in_dim(
                    matrix, part * inner_width + group * own_width, own_width, 1
                )
                for part in range(3)
            ],
            axis=1,
        )

    weight_mine = lax.all_gather(own_columns(w_qkv), REP, axis=0, tiled=True)
    latent_rows = gather_rep(latent)
    weight_grouped = by_group(w_qkv)
    b_grouped = by_group(b_qkv)
    weight_back = lax.all_gather(w_out, REP, axis=0, tiled=True)
    weight_in = lax.all_gather(weight_grouped, REP, axis=0, tiled=True)

    noise_level = timestep[0].astype(jnp.float32) / 1000.0
    mixed_in, normed = mix_in(latent_rows, noise[0], noise_level)
    sources, order = joined_all(normed, jnp.concatenate([weight_mine, a_qkv], axis=1))
    attended_heads, queries, keys, values, joined, lows = attend(
        order, sources, own_columns(b_qkv), text_kv, qk_gain
    )
    tokens = mixed_in.shape[0]
    attended = exchange(attended_heads.reshape(8, tokens, -1), SEQ)
    attended = jnp.transpose(attended, (1, 0, 2)).reshape(tokens, -1)
    low_out, patch_pre, partial_sum = project_out(
        attended, mixed_in, noise_level, weight_back, a_out, b_out, w_patch
    )
    summed = jnp.sum(spread(partial_sum, SEQ, 8), axis=0)
    pooled = summed / (tokens * 8)
    score_value, grad_pooled = jax.value_and_grad(reward)(pooled, prompt)
    grad_denoised, grad_attended, grad_a_out, grad_b_out = backward_out(
        patch_pre, grad_pooled, noise_level, attended, low_out, weight_back, a_out, b_out, w_patch
    )
    grad_heads = exchange(
        jnp.transpose(grad_attended.reshape(tokens, 8, -1), (1, 0, 2)), SEQ
    ).reshape(8 * tokens, -1)
    grad_joined, chunks = attend_back(
        group.reshape(1),
        joined,
        lows,
        qk_gain,
        queries,
        keys,
        values,
        attended_heads,
        grad_heads,
        (grad_a_out, grad_b_out),
    )
    grad_joined = exchange(grad_joined.reshape(8, tokens, -1), SEQ)
    early_half = halve(chunks.reshape(16, -1, chunks.shape[1]))
    rank = b_qkv.shape[0]
    grad_joined, grad_low, grad_a_qkv = low_back(grad_joined, b_grouped, normed)
    late_half = halve(grad_a_qkv)
    shard = sum_seq(scatter_chips(jnp.concatenate([early_half, late_half], axis=1)))
    early_shard, late_shard = shard[: early_half.shape[1]], shard[early_half.shape[1] :]
    late_rest = w_qkv.shape[0] - late_shard.shape[0]
    grad_normed = lax.dot_general(
        grad_joined, weight_in, contract_last, preferred_element_type=jnp.float32
    ) + lax.dot_general(grad_low, a_qkv, contract_last, preferred_element_type=jnp.float32)
    grad_mixed = jax.vjp(layer_norm, mixed_in)[1](grad_normed)[0] + grad_denoised
    grad_latent = (1.0 - noise_level) * grad_mixed
    latent_chunks = jnp.pad(grad_latent.reshape(16, 12, -1), ((0, 0), (0, 4), (0, 0)))
    latent_grad = scatter_chips(halve(latent_chunks))[:12]
    return (
        score_value.reshape(1),
        latent_grad,
        jnp.concatenate([late_shard[:, :rank], late_shard[:late_rest, rank:]], axis=0),
        early_shard[:, :rank].T,
        early_shard[:96, rank:],
        early_shard[96:248, rank:].T,
    )


def solution(mesh):
    parts = Mesh(mesh.devices.reshape(2, 4, 2, 4, 2), ("yh", "z", "core", "x", "yl"))
    in_specs = (
        P(SEQ + REP, None),
        P(REP, SEQ, None),
        P(REP),
        P(None, None, SEQ),
        P(),
        P(),
        P(REP, None),
        P(),
        P(),
        P(REP, None),
        P(),
        P(),
        P(),
    )
    out_specs = (
        P(REP),
        P(SEQ + REP, None),
        P(REP, None),
        P(None, REP),
        P(REP, None),
        P(None, REP),
    )
    return jax.shard_map(
        shards,
        mesh=parts,
        in_specs=in_specs,
        out_specs=out_specs,
        check_vma=False,
    )
```

```python
import math

import jax
import jax.numpy as jnp
from jax import lax
from jax.experimental import pallas as pl
from jax.experimental.pallas import tpu as pltpu
from jax.sharding import Mesh, PartitionSpec as P

HEAD_DIM = 64
CHIPS = ("yh", "z")
REP = ("yh", "z", "core")
SEQ = ("x", "yl")
QUERY_ROWS = 256
BACK_ROWS = 256
DOWN_ROWS = 80
LATENT_ROWS = 16


epsilon = 1e-06
logit_scale = 100.0
contract_last = (((1,), (1,)), ((), ()))
contract_first = (((0,), (0,)), ((), ()))


def layer_norm(mixed_in):
    centred = mixed_in - jnp.mean(mixed_in, axis=-1, keepdims=True)
    return centred * lax.rsqrt(jnp.mean(centred * centred, axis=-1, keepdims=True) + epsilon)


def mix_kernel(core, level, mine, other, noise, mixed, normed):
    size = 2 * mine.shape[1]
    first_core = core[0] == 0
    for chip in range(mine.shape[0]):
        ours, theirs = mine[chip].astype(jnp.float32), other[chip].astype(jnp.float32)
        rows = slice(chip * size, (chip + 1) * size)
        latent = jnp.concatenate(
            [jnp.where(first_core, ours, theirs), jnp.where(first_core, theirs, ours)], axis=0
        )
        block = (1.0 - level[0]) * latent + level[0] * noise[rows, :].astype(jnp.float32)
        mixed[rows, :] = block
        normed[rows, :] = layer_norm(block).astype(jnp.bfloat16)


def latent_kernel(core, level, product, down, low, mixed, grad_denoised, mine, other):
    size = mine.shape[1]
    first_core = core[0] == 0
    owned = mixed.shape[0] // 16
    for chip in range(mine.shape[0]):
        rows = slice(chip * 2 * owned, (chip + 1) * 2 * owned)
        grad = product[rows, :] + lax.dot_general(
            low[rows, :], down[...], contract_last, preferred_element_type=jnp.float32
        )
        block = mixed[rows, :]
        centred = block - jnp.mean(block, axis=-1, keepdims=True)
        inverse = lax.rsqrt(jnp.mean(centred * centred, axis=-1, keepdims=True) + epsilon)
        along = jnp.mean(centred * grad, axis=-1, keepdims=True) * inverse * inverse
        shifted = inverse * (grad - jnp.mean(grad, axis=-1, keepdims=True) - centred * along)
        grad_latent = (1.0 - level[0]) * (shifted + grad_denoised[rows, :])
        spare = jnp.zeros((size - owned, grad_latent.shape[1]), jnp.float32)
        first = jnp.concatenate([grad_latent[:owned], spare], axis=0)
        second = jnp.concatenate([grad_latent[owned:], spare], axis=0)
        mine[chip] = jnp.where(first_core, first, second)
        other[chip] = jnp.where(first_core, second, first).astype(jnp.bfloat16)


def head_means(width):
    rows = lax.broadcasted_iota(jnp.int32, (width, width), 0) // HEAD_DIM
    columns = lax.broadcasted_iota(jnp.int32, (width, width), 1) // HEAD_DIM
    return jnp.where(rows == columns, 1.0 / HEAD_DIM, 0.0).astype(jnp.bfloat16)


def mean_of(values, means):
    high = values.astype(jnp.bfloat16)
    low = (values - high.astype(jnp.float32)).astype(jnp.bfloat16)
    return jnp.dot(high, means, preferred_element_type=jnp.float32) + jnp.dot(
        low, means, preferred_element_type=jnp.float32
    )


def head_scale(values, gain, means):
    return values * lax.rsqrt(mean_of(values * values, means) + epsilon) * gain


def block_rows(sources, tokens):
    return [(ref, row) for ref in sources for row in range(0, ref.shape[0], tokens)]


def attend_kernel(
    order,
    near,
    middle,
    last,
    up,
    text,
    gain,
    attended,
    wide_queries,
    queries,
    keys,
    values,
    joined,
    lows,
    widened,
):
    heads, latents = queries.shape[0], queries.shape[1]
    tokens, width = last.shape[0], joined.shape[2]
    texts = text.shape[1]
    means = head_means(width)

    def by_head(target, rows, matrix):
        for head in range(heads):
            target[head, rows, :] = matrix[:, head * HEAD_DIM : (head + 1) * HEAD_DIM]

    for at, (source, row) in enumerate(block_rows((near, middle, last), tokens)):
        rows = pl.ds(pl.multiple_of(order[at] * tokens, tokens), tokens)
        low = source[row : row + tokens, 3 * width :].astype(jnp.bfloat16)
        block = source[row : row + tokens, : 3 * width] + jnp.dot(
            low, up[...], preferred_element_type=jnp.float32
        )
        lows[rows, :] = low
        query, key = block[:, :width], block[:, width : 2 * width]
        joined[0, rows, :] = query
        joined[1, rows, :] = key
        scaled = head_scale(query, gain[0:1, :], means).astype(jnp.bfloat16)
        wide_queries[rows, :] = scaled
        by_head(queries, rows, scaled)
        by_head(keys, rows, head_scale(key, gain[1:2, :], means).astype(jnp.bfloat16))
        by_head(values, rows, block[:, 2 * width :].astype(jnp.bfloat16))
    rows = slice(latents, latents + texts)
    text_key = text[0].astype(jnp.float32)
    by_head(keys, rows, head_scale(text_key, gain[1:2, :], means).astype(jnp.bfloat16))
    by_head(values, rows, text[1])
    for head in range(heads):
        lanes = lax.broadcasted_iota(jnp.int32, (latents + texts, HEAD_DIM), 1)
        ones = jnp.where(lanes == 0, 1.0, 0.0).astype(jnp.bfloat16)
        widened[head] = jnp.concatenate([values[head], ones], axis=1)

    def block(at, carry):
        rows = pl.ds(pl.multiple_of(at * QUERY_ROWS, QUERY_ROWS), QUERY_ROWS)
        parts = []
        for head in range(heads):
            logits = lax.dot_general(
                queries[head, rows, :], keys[head], contract_last, preferred_element_type=jnp.float32
            )
            expped = jnp.exp(logits * (1.0 / math.sqrt(HEAD_DIM))).astype(jnp.bfloat16)
            summed = jnp.dot(expped, widened[head], preferred_element_type=jnp.float32)
            parts.append(summed[:, :HEAD_DIM] / summed[:, HEAD_DIM : HEAD_DIM + 1])
        attended[rows, :] = jnp.concatenate(parts, axis=1).astype(jnp.bfloat16)
        return carry

    lax.fori_loop(0, latents // QUERY_ROWS, block, 0)


def attend_back_kernel(
    group,
    joined,
    lows,
    gain,
    wide_queries,
    queries,
    keys,
    values,
    attended,
    grads,
    grad_a_out,
    grad_b_out,
    grad_joined,
    chunks,
    key_columns,
    grad_queries,
    grad_keys,
    grad_values,
):
    heads, latents = queries.shape[0], queries.shape[1]
    tokens, width, rank = latents // 8, joined.shape[2], lows.shape[1]
    lane_head = lax.broadcasted_iota(jnp.int32, (1, width), 1) // HEAD_DIM
    indicator = jnp.where(
        lax.broadcasted_iota(jnp.int32, (8, width), 0)
        == lax.broadcasted_iota(jnp.int32, (8, width), 1) // HEAD_DIM,
        1.0,
        0.0,
    ).astype(jnp.float32)
    for head in range(heads):
        key_columns[head] = keys[head].astype(jnp.float32).T.astype(jnp.bfloat16)
    grad_keys[...] = jnp.zeros(grad_keys.shape, jnp.float32)
    grad_values[...] = jnp.zeros(grad_values.shape, jnp.float32)

    def own_lanes(matrix):
        zero = jnp.zeros(matrix.shape, matrix.dtype)
        return jnp.concatenate(
            [jnp.where(lane_head == head, matrix, zero) for head in range(heads)], axis=0
        )

    def block(at, carry):
        rows = pl.ds(pl.multiple_of(at * BACK_ROWS, BACK_ROWS), BACK_ROWS)
        grad_rows = grads[rows, :]
        products = attended[rows, :].astype(jnp.float32) * grad_rows.astype(jnp.float32)
        centres = lax.dot_general(
            indicator,
            products,
            contract_last,
            precision=lax.Precision.HIGHEST,
            preferred_element_type=jnp.float32,
        )
        all_probs, all_logits, columns = [], [], []
        for head in range(heads):
            left, right = head * HEAD_DIM, (head + 1) * HEAD_DIM
            logits = lax.dot_general(
                keys[head],
                queries[head, rows, :],
                contract_last,
                preferred_element_type=jnp.float32,
            )
            expped = jnp.exp(logits * (1.0 / math.sqrt(HEAD_DIM)))
            probs = expped * (1.0 / jnp.sum(expped, axis=0, keepdims=True))
            grad_probs = lax.dot_general(
                values[head],
                grad_rows[:, left:right],
                contract_last,
                preferred_element_type=jnp.float32,
            )
            grad_logits = (probs * (grad_probs - centres[head : head + 1, :])).astype(jnp.bfloat16)
            columns.append(
                jnp.dot(key_columns[head], grad_logits, preferred_element_type=jnp.float32)
            )
            all_probs.append(probs[:latents].astype(jnp.bfloat16))
            all_logits.append(grad_logits[:latents])
        grad_queries[rows, :] = jnp.concatenate(columns, axis=0).T
        grad_values[...] += jnp.dot(
            jnp.concatenate(all_probs, axis=1),
            own_lanes(grad_rows),
            preferred_element_type=jnp.float32,
        )
        grad_keys[...] += jnp.dot(
            jnp.concatenate(all_logits, axis=1),
            own_lanes(wide_queries[rows, :]),
            preferred_element_type=jnp.float32,
        )
        return carry

    lax.fori_loop(0, latents // BACK_ROWS, block, 0)

    scale, means = 1.0 / math.sqrt(HEAD_DIM), head_means(width)
    grad_up = jnp.zeros((rank, 3 * width), jnp.float32)
    for at in range(8):
        rows = slice(at * tokens, (at + 1) * tokens)
        parts = []
        for part, sums in enumerate((grad_queries, grad_keys)):
            inputs = joined[part, rows, :]
            incoming = (sums[rows, :] * scale).astype(jnp.bfloat16).astype(jnp.float32)
            incoming = incoming * gain[part : part + 1, :]
            inverse = lax.rsqrt(mean_of(inputs * inputs, means) + epsilon)
            along = mean_of(inputs * incoming, means)
            parts.append(inverse * incoming - inputs * (inverse * inverse * inverse * along))
        parts.append(grad_values[rows, :])
        result = jnp.concatenate(parts, axis=1).astype(jnp.bfloat16)
        grad_up += lax.dot_general(
            lows[rows, :], result, contract_first, preferred_element_type=jnp.float32
        )
        grad_joined[rows, :] = result
    grad_up = grad_up.T

    chunks[...] = jnp.zeros(chunks.shape, jnp.bfloat16)
    for part in range(3):
        place = pl.ds(pl.multiple_of(part * latents + group[0] * width, width), width)
        chunks[place, 0:rank] = grad_up[part * width : (part + 1) * width].astype(jnp.bfloat16)
    size, first, second = (ref.shape[0] // 16 for ref in (chunks, grad_a_out, grad_b_out))
    for replica in range(16):
        at = replica * size
        chunks[at : at + first, rank:] = grad_a_out[
            replica * first : (replica + 1) * first, :
        ].astype(jnp.bfloat16)
        chunks[at + first : at + first + second, rank:] = grad_b_out[
            replica * second : (replica + 1) * second, :
        ].astype(jnp.bfloat16)


def low_back_kernel(grad_joined, up, normed, flat, grad_low, grad_down):
    for group in range(0, grad_joined.shape[0], 2):
        pair = jnp.concatenate([grad_joined[group], grad_joined[group + 1]], axis=1)
        flat[:, group // 2 * pair.shape[1] : (group // 2 + 1) * pair.shape[1]] = pair
    low = lax.dot_general(
        flat[...], up[...], contract_last, preferred_element_type=jnp.float32
    ).astype(jnp.bfloat16)
    grad_low[...] = low
    down = lax.dot_general(normed[...], low, contract_first, preferred_element_type=jnp.float32)
    replicas, rows, lanes = grad_down.shape
    size, rank = down.shape[0] // replicas, down.shape[1]
    grad_down[...] = jnp.zeros(grad_down.shape, jnp.float32)
    for replica in range(replicas):
        at = replica * size
        grad_down[replica, :, 0:rank] = down[at : at + rows]
        grad_down[replica, 0 : size - rows, rank:lanes] = down[at + rows : at + size]


def in_vmem(count):
    return [pl.BlockSpec(memory_space=pltpu.VMEM)] * count


def in_smem(count):
    return [pl.BlockSpec(memory_space=pltpu.SMEM)] * count


def mix(core, level, mine, other, noise):
    return pl.pallas_call(
        mix_kernel,
        name="mix",
        out_shape=(
            jax.ShapeDtypeStruct(noise.shape, jnp.float32),
            jax.ShapeDtypeStruct(noise.shape, jnp.bfloat16),
        ),
        in_specs=in_smem(2) + in_vmem(3),
        out_specs=tuple(in_vmem(2)),
    )(core, level, mine, other, noise)


def latent_split(core, level, product, down, low, mixed, grad_denoised):
    shape = (8, LATENT_ROWS, mixed.shape[1])
    return pl.pallas_call(
        latent_kernel,
        name="latent_split",
        out_shape=(
            jax.ShapeDtypeStruct(shape, jnp.float32),
            jax.ShapeDtypeStruct(shape, jnp.bfloat16),
        ),
        in_specs=in_smem(2) + in_vmem(5),
        out_specs=tuple(in_vmem(2)),
    )(core, level, product, down, low, mixed, grad_denoised)


def attend(order, sources, up, text_kv, gain):
    latents, rank, width = 8 * sources[-1].shape[0], up.shape[0], up.shape[1]
    heads = width // (3 * HEAD_DIM)
    everything = latents + text_kv.shape[1]
    return pl.pallas_call(
        attend_kernel,
        name="attend",
        out_shape=(
            jax.ShapeDtypeStruct((latents, heads * HEAD_DIM), jnp.bfloat16),
            jax.ShapeDtypeStruct((latents, heads * HEAD_DIM), jnp.bfloat16),
            jax.ShapeDtypeStruct((heads, latents, HEAD_DIM), jnp.bfloat16),
            jax.ShapeDtypeStruct((heads, everything, HEAD_DIM), jnp.bfloat16),
            jax.ShapeDtypeStruct((heads, everything, HEAD_DIM), jnp.bfloat16),
            jax.ShapeDtypeStruct((2, latents, width // 3), jnp.float32),
            jax.ShapeDtypeStruct((latents, rank), jnp.bfloat16),
        ),
        in_specs=[pl.BlockSpec(memory_space=pltpu.SMEM)] + in_vmem(6),
        out_specs=tuple(in_vmem(7)),
        scratch_shapes=[pltpu.VMEM((heads, everything, 2 * HEAD_DIM), jnp.bfloat16)],
    )(order, *sources, up, text_kv, gain)


def attend_back(group, joined, lows, gain, projected, attended, grads, out_grads):
    latents, rank, width = lows.shape[0], lows.shape[1], 3 * joined.shape[2]
    heads, everything = projected[2].shape[0], projected[2].shape[1]
    return pl.pallas_call(
        attend_back_kernel,
        name="attend_back",
        out_shape=(
            jax.ShapeDtypeStruct((latents, width), jnp.bfloat16),
            jax.ShapeDtypeStruct((8 * width, 2 * rank), jnp.bfloat16),
        ),
        in_specs=in_smem(1) + in_vmem(11),
        out_specs=tuple(in_vmem(2)),
        scratch_shapes=[
            pltpu.VMEM((heads, HEAD_DIM, everything), jnp.bfloat16),
            pltpu.VMEM((latents, heads * HEAD_DIM), jnp.float32),
            pltpu.VMEM((latents, heads * HEAD_DIM), jnp.float32),
            pltpu.VMEM((latents, heads * HEAD_DIM), jnp.float32),
        ],
    )(group, joined, lows, gain, *projected, attended, grads, *out_grads)


def low_back(grad_joined, up, normed):
    groups, tokens, width = grad_joined.shape
    return pl.pallas_call(
        low_back_kernel,
        name="low_back",
        out_shape=(
            jax.ShapeDtypeStruct((tokens, groups * width), jnp.bfloat16),
            jax.ShapeDtypeStruct((tokens, up.shape[0]), jnp.bfloat16),
            jax.ShapeDtypeStruct((16, DOWN_ROWS, 2 * up.shape[0]), jnp.float32),
        ),
        in_specs=in_vmem(3),
        out_specs=tuple(in_vmem(3)),
    )(grad_joined, up, normed)


def project_out(attended, mixed_in, noise_level, w_out, a_out, b_out, w_patch):
    low_out = jnp.dot(attended, a_out, preferred_element_type=jnp.float32).astype(jnp.bfloat16)
    velocity = jnp.dot(attended, w_out, preferred_element_type=jnp.float32) + jnp.dot(
        low_out, b_out, preferred_element_type=jnp.float32
    )
    denoised = (mixed_in - noise_level * velocity).astype(jnp.bfloat16)
    patch_pre = jnp.dot(denoised, w_patch, preferred_element_type=jnp.float32)
    return (low_out, patch_pre, jnp.sum(jax.nn.gelu(patch_pre), axis=0))


def reward(pooled, prompt):
    return (
        logit_scale
        * jnp.sum(pooled * prompt)
        * lax.rsqrt(jnp.sum(pooled * pooled) + epsilon)
        * lax.rsqrt(jnp.sum(prompt * prompt) + epsilon)
    )


def backward_out(
    patch_pre, grad_pooled, noise_level, attended, low_out, w_out, a_out, b_out, w_patch
):
    gelu_back = jax.vjp(jax.nn.gelu, patch_pre)[1]
    grad_pre = gelu_back(jnp.broadcast_to(grad_pooled, patch_pre.shape))[0].astype(jnp.bfloat16)
    grad_denoised = lax.dot_general(
        grad_pre, w_patch, contract_last, preferred_element_type=jnp.float32
    )
    grad_velocity = (-noise_level * grad_denoised).astype(jnp.bfloat16)
    grad_low_out = lax.dot_general(
        grad_velocity, b_out, contract_last, preferred_element_type=jnp.float32
    ).astype(jnp.bfloat16)
    grad_attended = (
        lax.dot_general(grad_velocity, w_out, contract_last, preferred_element_type=jnp.float32)
        + lax.dot_general(grad_low_out, a_out, contract_last, preferred_element_type=jnp.float32)
    ).astype(jnp.bfloat16)
    grad_a_out = lax.dot_general(
        attended, grad_low_out, contract_first, preferred_element_type=jnp.float32
    )
    grad_b_out = lax.dot_general(
        grad_velocity, low_out, contract_first, preferred_element_type=jnp.float32
    )
    return (grad_denoised, grad_attended, grad_a_out, grad_b_out)


def shift(block, axis, step, size):
    return lax.ppermute(block, axis, [(i, (i + step) % size) for i in range(size)])


def exchange(blocks, axes):
    return lax.all_to_all(blocks, axes, split_axis=0, concat_axis=0, tiled=True)


def spread(block, axes, size):
    return exchange(jnp.broadcast_to(block[None], (size,) + block.shape), axes)


def add_swapped(mine, other):
    got = shift(other.astype(jnp.bfloat16), "core", 1, 2)
    return (mine.astype(jnp.float32) + got.astype(jnp.float32)).astype(jnp.bfloat16)


def halve(chunks):
    pairs = chunks.reshape((8, 2) + chunks.shape[1:])
    core = lax.axis_index("core")
    mine = lax.dynamic_index_in_dim(pairs, core, 1, keepdims=False)
    other = lax.dynamic_index_in_dim(pairs, 1 - core, 1, keepdims=False)
    return add_swapped(mine, other)


def scatter_chips(half):
    parts = exchange(half, CHIPS)
    return jnp.sum(parts.astype(jnp.float32), axis=0)


def sum_seq(block):
    for axis, size, distance in (("yl", 2, 1), ("x", 4, 1), ("x", 4, 2)):
        sent = block.astype(jnp.bfloat16)
        got = lax.ppermute(sent, axis, [(i, i ^ distance) for i in range(size)])
        block = sent.astype(jnp.float32) + got.astype(jnp.float32)
    return block


def joined_all(rows, weight):
    third = rows.shape[0] // 3
    before = shift(rows, "x", 1, 4)
    after = shift(rows, "x", -1, 4)
    beside = shift(rows, "yl", 1, 2)
    far = shift(before, "x", 1, 4)
    after_beside = shift(beside, "x", -1, 4)
    before_beside = shift(before, "yl", 1, 2)
    near = jnp.concatenate([rows, before, after, beside], axis=0)
    near = jnp.dot(near, weight, preferred_element_type=jnp.float32)
    far, after_beside, before_beside, near = lax.optimization_barrier(
        (far, after_beside, before_beside, near)
    )
    opposite = [
        shift(before_beside[:third], "x", 1, 4),
        shift(after_beside[third : 2 * third], "x", -1, 4),
        shift(far[2 * third :], "yl", 1, 2),
    ]
    middle = jnp.concatenate([far, after_beside, before_beside], axis=0)
    middle = jnp.dot(middle, weight, preferred_element_type=jnp.float32)
    *opposite, middle = lax.optimization_barrier((*opposite, middle))
    last = jnp.concatenate(opposite, axis=0)
    last = jnp.dot(last, weight, preferred_element_type=jnp.float32)
    at_x, at_y = lax.axis_index("x"), lax.axis_index("yl")
    steps = ((0, 0), (3, 0), (1, 0), (0, 1), (2, 0), (1, 1), (3, 1), (2, 1))
    order = jnp.stack([((at_x + x) % 4) * 2 + (at_y + y) % 2 for x, y in steps])
    return ((near, middle, last), order.astype(jnp.int32))


def place_kernel(places, *refs):
    *blocks, others, target = refs
    rows = blocks[0].shape[0]
    for at, block in enumerate(blocks):
        mine = pl.ds(pl.multiple_of(places[at] * rows, rows), rows)
        theirs = pl.ds(pl.multiple_of(places[8 + at] * rows, rows), rows)
        target[mine, :] = block[...]
        target[theirs, :] = others[at * rows : (at + 1) * rows, :]


def gather_out(block):
    before = shift(block, "z", 1, 4)
    after = shift(block, "z", -1, 4)
    beside = shift(block, "yh", 1, 2)
    far = shift(before, "z", 1, 4)
    before_beside = shift(beside, "z", 1, 4)
    after_beside = shift(beside, "z", -1, 4)
    far_beside = shift(after_beside, "z", -1, 4)
    blocks = (block, before, after, beside, far, before_beside, after_beside, far_beside)
    steps = ((0, 0), (3, 0), (1, 0), (0, 1), (2, 0), (3, 1), (1, 1), (2, 1))
    others = shift(jnp.concatenate(blocks, axis=0), "core", 1, 2)
    at_y, at_z, core = lax.axis_index("yh"), lax.axis_index("z"), lax.axis_index("core")
    chips = [((at_y + y) % 2) * 4 + (at_z + z) % 4 for z, y in steps]
    places = jnp.stack([chip * 2 + core for chip in chips] + [chip * 2 + 1 - core for chip in chips])
    return pl.pallas_call(
        place_kernel,
        name="place",
        out_shape=jax.ShapeDtypeStruct((16 * block.shape[0], block.shape[1]), block.dtype),
        in_specs=in_smem(1) + in_vmem(9),
        out_specs=pl.BlockSpec(memory_space=pltpu.VMEM),
    )(places.astype(jnp.int32), *blocks, others)


def by_group(columns):
    rows = columns.shape[0]
    return jnp.transpose(columns.reshape(rows, 3, 8, -1), (0, 2, 1, 3)).reshape(rows, -1)


def shards(
    latent,
    noise,
    timestep,
    text_kv,
    qk_gain,
    prompt,
    w_qkv,
    a_qkv,
    b_qkv,
    w_out,
    a_out,
    b_out,
    w_patch,
):
    group = lax.axis_index("x") * 2 + lax.axis_index("yl")
    inner_width, own_width = w_qkv.shape[1] // 3, w_qkv.shape[1] // 24

    def own_columns(matrix):
        return jnp.concatenate(
            [
                lax.dynamic_slice_in_dim(
                    matrix, part * inner_width + group * own_width, own_width, 1
                )
                for part in range(3)
            ],
            axis=1,
        )

    weight_own, latent = lax.optimization_barrier((own_columns(w_qkv), latent))
    weight_mine = lax.all_gather(weight_own, REP, axis=0, tiled=True)
    latent_mine = spread(latent, CHIPS, 8)
    latent_other = shift(latent_mine, "core", 1, 2)
    weight_grouped = by_group(w_qkv)
    b_grouped = by_group(b_qkv)
    weight_back = gather_out(w_out)
    weight_in = lax.all_gather(weight_grouped, REP, axis=0, tiled=True)

    noise_level = timestep[0].astype(jnp.float32) / 1000.0
    core, level = lax.axis_index("core").reshape(1).astype(jnp.int32), noise_level.reshape(1)
    mixed_in, normed = mix(core, level, latent_mine, latent_other, noise[0])
    sources, order = joined_all(normed, jnp.concatenate([weight_mine, a_qkv], axis=1))
    gain = jnp.tile(qk_gain, (1, own_width // HEAD_DIM))
    attended_heads, *projected, joined, lows = attend(
        order, sources, own_columns(b_qkv), text_kv, gain
    )
    tokens = mixed_in.shape[0]
    attended = exchange(attended_heads.reshape(8, tokens, -1), SEQ)
    attended = jnp.transpose(attended, (1, 0, 2)).reshape(tokens, -1)
    low_out, patch_pre, partial_sum = project_out(
        attended, mixed_in, noise_level, weight_back, a_out, b_out, w_patch
    )
    summed = jnp.sum(spread(partial_sum, SEQ, 8), axis=0)
    pooled = summed / (tokens * 8)
    score_value, grad_pooled = jax.value_and_grad(reward)(pooled, prompt)
    grad_denoised, grad_attended, grad_a_out, grad_b_out = backward_out(
        patch_pre, grad_pooled, noise_level, attended, low_out, weight_back, a_out, b_out, w_patch
    )
    grad_heads = exchange(
        jnp.transpose(grad_attended.reshape(tokens, 8, -1), (1, 0, 2)), SEQ
    ).reshape(8 * tokens, -1)
    grad_joined, chunks = attend_back(
        group.reshape(1),
        joined,
        lows,
        gain,
        projected,
        attended_heads,
        grad_heads,
        (grad_a_out, grad_b_out),
    )
    grad_joined = exchange(grad_joined.reshape(8, tokens, -1), SEQ)
    early_half = halve(chunks.reshape(16, -1, chunks.shape[1]))
    rank = b_qkv.shape[0]
    grad_joined, grad_low, grad_a_qkv = low_back(grad_joined, b_grouped, normed)
    late_half = halve(grad_a_qkv)
    shard = sum_seq(scatter_chips(jnp.concatenate([early_half, late_half], axis=1)))
    early_shard, late_shard = shard[: early_half.shape[1]], shard[early_half.shape[1] :]
    late_rest = w_qkv.shape[0] - late_shard.shape[0]
    grad_normed = lax.dot_general(
        grad_joined, weight_in, contract_last, preferred_element_type=jnp.float32
    )
    halves = latent_split(core, level, grad_normed, a_qkv, grad_low, mixed_in, grad_denoised)
    latent_grad = scatter_chips(add_swapped(*halves))[: latent.shape[0]]
    return (
        score_value.reshape(1),
        latent_grad,
        jnp.concatenate([late_shard[:, :rank], late_shard[:late_rest, rank:]], axis=0),
        early_shard[:, :rank].T,
        early_shard[:96, rank:],
        early_shard[96:248, rank:].T,
    )


def solution(mesh):
    parts = Mesh(mesh.devices.reshape(2, 4, 2, 4, 2), ("yh", "z", "core", "x", "yl"))
    in_specs = (
        P(SEQ + REP, None),
        P(REP, SEQ, None),
        P(REP),
        P(None, None, SEQ),
        P(),
        P(),
        P(REP, None),
        P(),
        P(),
        P(REP, None),
        P(),
        P(),
        P(),
    )
    out_specs = (
        P(REP),
        P(SEQ + REP, None),
        P(REP, None),
        P(None, REP),
        P(REP, None),
        P(None, REP),
    )
    return jax.shard_map(
        shards,
        mesh=parts,
        in_specs=in_specs,
        out_specs=out_specs,
        check_vma=False,
    )
```
